32 devices in a mesh: groups: 2 (over x), expert: 8 (over z, y), dp: 2 (over core).
Axes of the slice: x: 2, y: 2, z: 4, core: 2. Of those that a mesh axis runs over, the one named last changes fastest.
Arguments:
- captured: bfloat16 [32768, 1536], P(('groups', 'expert', 'dp')), parts along dimension 0, may hold values from -16 to 16
- routes: int32 [32768, 1], P(('groups', 'expert', 'dp')), parts along dimension 0, may hold values from 0 to 15; in each aligned block of 1024 rows (0 to 1023, 1024 to 2047, ...) at most 80 rows name the same one
Outputs:
- hessians: float32 [32, 1536, 1536], P(('groups', 'expert'), 'dp'), parts along dimension 0
The draws below stay inside these ranges and needn't reach their ends.
There are 2 independent parts, one for each index of `groups`. The reference program is written for one: setup_inputs(seed, part) draws one part's arguments, and reference() takes and returns one part's arrays. A program takes and returns all parts, laid end to end along the dimension named above; each array names one. Nothing has to cross between parts.
Inputs may be any that keep to these rules, and one draw needn't show every extreme that they name: `routes`: among the rows of one device no expert is named by more than 80 rows; every expert is named by some row of the part.
All inputs are finite; a program needn't handle non-finite values.
Results may differ from the reference program's by a relative error of at most 0.0003.
Values may be sent and summed in bfloat16 or wider, within the bound.
No kernel may reach another device: no remote copies, remote signals or barrier semaphores. Data moves between devices by JAX's collectives and lax.ppermute only.
A program may use at most 64 MiB of HBM per device.

```python
import math
import jax
import jax.numpy as jnp
import numpy as np
from jax import lax

F = 1536
ROWS_DEV = 1024
EXPERTS = 16
CAP = 80
ROWS = 16384
N_EXPERT = 8
N_DP = 2


def draw_captured(key, part):
    key_base = jax.random.fold_in(key, 11)
    key_cols = jax.random.fold_in(key, 12)
    key_rows = jax.random.fold_in(key, 13)
    position = jnp.arange(F, dtype=jnp.float32) / jnp.float32(F - 1)
    col_lo, col_hi, row_lo, row_hi = (0.5, 2.0, 0.6, 1.6)
    base = jax.random.normal(key_base, (ROWS, F), jnp.float32)
    col_scale = col_lo * (col_hi / col_lo) ** position
    col_scale = col_scale * jnp.exp(jax.random.uniform(key_cols, (F,), jnp.float32, -0.35, 0.35))
    row_scale = jnp.exp(jax.random.uniform(key_rows, (ROWS, 1), jnp.float32, jnp.log(row_lo), jnp.log(row_hi)))
    values = jnp.clip(base * col_scale[None, :] * row_scale, -16.0, 16.0)
    return values.astype(jnp.bfloat16)


def deal_out(rng, own, number, rows, amount, top, limit, skew):
    order = jax.random.permutation(rng, amount)
    crowded, ordinary = load_shares(amount, rows * top, limit, skew, True), load_shares(amount, rows * top, limit, skew, False)
    places = jnp.arange(amount)

    def named(lengths, turn):
        used = int((lengths > 0).sum())
        fixed = max(1, used // 4)
        passed = fixed + (places - fixed + turn * (used - fixed)) % max(1, amount - fixed)
        return jnp.zeros((amount,), jnp.int32).at[order[jnp.where(places < fixed, places, passed)]].set(jnp.asarray(lengths, jnp.int32))

    lengths = jnp.where(number % 4 == 0, named(crowded, number // 4), named(ordinary, number - number // 4 - 1))
    mixed = jax.random.permutation(jax.random.fold_in(own, 3), amount)
    giver, receiver = mixed[0:amount // 2 * 2:2], mixed[1:amount // 2 * 2:2]
    slack = jnp.minimum(lengths[giver] - 1, limit - lengths[receiver]) // 2
    slack = jnp.where((giver == order[0]) | (receiver == order[0]) | (lengths[receiver] == 0), 0, jnp.maximum(slack, 0))
    passed = jax.random.randint(jax.random.fold_in(own, 4), (amount // 2,), 0, 1 << 20) % (slack + 1)
    lengths = lengths.at[giver].add(-passed).at[receiver].add(passed)
    labels = jnp.searchsorted(jnp.cumsum(lengths), jnp.arange(rows * top), side="right").astype(jnp.int32)
    grid = labels.reshape(top, rows).T
    grid = grid[jax.random.permutation(jax.random.fold_in(own, 1), rows)]
    turn = jax.random.randint(jax.random.fold_in(own, 2), (rows, 1), 0, top)
    return jnp.take_along_axis(grid, (jnp.arange(top)[None, :] + turn) % top, axis=1)


def load_shares(number_of, total, bound, lean, full):
    weights = [(1 << 20) // math.isqrt(grade ** lean) + 1 for grade in range(1, number_of + 1)]
    largest = bound if full else min(bound, max(-(-total // number_of), total * weights[0] // sum(weights)))
    least = 1 if total - largest >= number_of - 1 else 0
    given, surplus = [largest] + [least] * (number_of - 1), total - largest - least * (number_of - 1)
    while surplus > 0:
        candidates = [i for i in range(1, number_of) if given[i] < largest] or [i for i in range(1, number_of) if given[i] < bound]
        whole, budget = sum([weights[i] for i in candidates]), surplus
        for i in candidates:
            extra = min(bound - given[i], max(1, budget * weights[i] // whole), surplus)
            given[i] = given[i] + extra
            surplus = surplus - extra
    return np.array(given)


def setup_inputs(seed: int = 0, part: int = 0) -> dict:
    key_of = jax.random.split(jax.random.key(seed), 3)
    part_keys = jax.random.split(jax.random.fold_in(key_of[2], part), 3)
    captured = draw_captured(jax.random.fold_in(jax.random.fold_in(key_of[2], part), 71), part)
    routes_keys = jax.random.split(jax.random.fold_in(part_keys[1], 1), ROWS // ROWS_DEV)
    routes_turns = jax.random.permutation(jax.random.fold_in(part_keys[1], 3), ROWS // ROWS_DEV)
    routes = jax.vmap(lambda own, number: deal_out(jax.random.fold_in(part_keys[1], 2), own, number, ROWS_DEV, EXPERTS, 1, CAP, 2))(routes_keys, routes_turns).reshape((ROWS, 1))
    return {"captured": captured, "routes": routes}


def reference(captured, routes):
    expert_ids = routes[:, 0].astype(jnp.int32)
    sorted_order = jnp.argsort(expert_ids, stable=True)
    ordered = captured[sorted_order]
    counts = jnp.sum((expert_ids[:, None] == jnp.arange(EXPERTS, dtype=jnp.int32)[None, :]).astype(jnp.int32), axis=0)
    offsets = (jnp.cumsum(counts) - counts).astype(jnp.int32)
    most_rows = N_EXPERT * N_DP * CAP
    padded = jnp.concatenate([ordered, jnp.zeros((most_rows, F), ordered.dtype)], axis=0)
    unit_rows = jnp.eye(F, dtype=jnp.float32)

    def per_expert(index):
        row_block = lax.dynamic_slice_in_dim(padded, offsets[index].astype(jnp.int32), most_rows, 0)
        live_rows = jnp.arange(most_rows) < counts[index]
        row_block = jnp.where(live_rows[:, None], row_block, jnp.zeros_like(row_block))
        gram_full = jnp.dot(row_block.T, row_block, preferred_element_type=jnp.float32)
        scaled = gram_full * (2.0 / counts[index].astype(jnp.float32))
        damping = 0.1 * jnp.mean(jnp.diagonal(scaled))
        return scaled + damping * unit_rows

    return lax.map(per_expert, jnp.arange(EXPERTS, dtype=jnp.int32))
```

```python
import functools

import jax
import jax.numpy as jnp
from jax import lax
from jax.experimental import pallas as pl
from jax.experimental.pallas import tpu as pltpu
from jax.sharding import PartitionSpec as P

EXP_DEV = 2
LANES = 128
EMPTY = 64.0


def slot_codes(routes, experts, capacity):
    blocks = routes.shape[0]
    hits = [routes == expert for expert in range(experts)]
    onehot = jnp.concatenate([hit.astype(jnp.float32) for hit in hits], axis=0).astype(jnp.bfloat16)
    rows = lax.broadcasted_iota(jnp.int32, (LANES, LANES), 0)
    cols = lax.broadcasted_iota(jnp.int32, (LANES, LANES), 1)
    upto = jnp.where(rows <= cols, 1.0, 0.0).astype(jnp.bfloat16)
    ones = jnp.ones((LANES, LANES), jnp.bfloat16)
    within = jnp.dot(onehot, upto, preferred_element_type=jnp.float32)
    totals = jnp.dot(onehot, ones, preferred_element_type=jnp.float32).astype(jnp.bfloat16)
    side = experts * blocks
    left = lax.broadcasted_iota(jnp.int32, (side, side), 0)
    right = lax.broadcasted_iota(jnp.int32, (side, side), 1)
    same = (left // blocks == right // blocks) & (right < left)
    before = jnp.where(same, 1.0, 0.0).astype(jnp.bfloat16)
    rank = within + jnp.dot(before, totals, preferred_element_type=jnp.float32) - 1.0
    code = jnp.zeros(routes.shape, jnp.float32)
    for expert in range(experts):
        own = rank[expert * blocks : (expert + 1) * blocks]
        code = jnp.where(hits[expert], own + float(expert * capacity), code)
    return code.astype(jnp.int32)


def select_rows(code, owners, slots, captured, out_refs):
    blocks = code.shape[0]
    picks = []
    for owner in owners:
        wanted = lax.broadcasted_iota(jnp.int32, (slots, LANES), 0) + owner * slots
        row = [
            jnp.where(code[block : block + 1] == wanted, 1.0, 0.0).astype(jnp.bfloat16)
            for block in range(blocks)
        ]
        picks.append(jnp.concatenate(row, axis=1))
    pick = jnp.concatenate(picks, axis=0)
    packed = jnp.dot(pick, captured, preferred_element_type=jnp.float32).astype(jnp.bfloat16)
    ones = jnp.ones((captured.shape[0], LANES), jnp.bfloat16)
    filled = jnp.dot(pick, ones, preferred_element_type=jnp.float32)
    lane = lax.broadcasted_iota(jnp.int32, filled.shape, 1)
    empty = (filled < 0.5) & (lane == 0)
    head = jnp.where(empty, EMPTY, packed[:, :LANES].astype(jnp.float32)).astype(jnp.bfloat16)
    for i, out_ref in enumerate(out_refs):
        out_ref[:, :LANES] = head[i * slots : (i + 1) * slots]
        out_ref[:, LANES:] = packed[i * slots : (i + 1) * slots, LANES:]


def pack_kernel(offsets, experts, capacity, me_ref, routes_ref, captured_ref, *out_refs):
    code = slot_codes(routes_ref[...], experts, capacity)
    owners = [me_ref[0] ^ offset for offset in offsets]
    select_rows(code, owners, EXP_DEV * capacity, captured_ref[...], out_refs)


def pack(offsets, experts, capacity, me, routes, captured):
    rows, width = captured.shape
    slots = EXP_DEV * capacity
    out = jax.ShapeDtypeStruct((slots, width), captured.dtype)
    vmem = pl.BlockSpec(memory_space=pltpu.VMEM)
    return pl.pallas_call(
        functools.partial(pack_kernel, offsets, experts, capacity),
        out_shape=[out] * len(offsets),
        in_specs=[pl.BlockSpec(memory_space=pltpu.SMEM), vmem, vmem],
        out_specs=[vmem] * len(offsets),
        cost_estimate=pl.CostEstimate(
            flops=2 * len(offsets) * slots * rows * width,
            bytes_accessed=2 * width * (rows + len(offsets) * slots),
            transcendentals=0,
        ),
        name="pack",
    )(me, routes, captured)


def hessian_kernel(parts, capacity, half, tile, side_ref, *refs):
    chunk_refs, out_ref, rows_ref, stat_ref, sems = refs[:parts], refs[parts], *refs[parts + 1 :]
    width = rows_ref.shape[2]
    tiles = half // tile
    step = pl.program_id(0)
    local = step // tiles
    place = lax.rem(step, tiles)

    def copy(expert, part):
        return pltpu.make_async_copy(
            chunk_refs[part].at[pl.ds(expert * capacity, capacity)],
            rows_ref.at[expert, pl.ds(part * capacity, capacity)],
            sems.at[expert, part],
        )

    @pl.when(step == 0)
    def _():
        for expert in range(EXP_DEV):
            for part in range(parts):
                copy(expert, part).start()

    for expert in range(EXP_DEV):

        @pl.when(step == expert * tiles)
        def _():
            for part in range(parts):
                copy(expert, part).wait()
            head = rows_ref[expert, :, :LANES].astype(jnp.float32)
            empty = head > 0.5 * EMPTY
            rows_ref[expert, :, :LANES] = jnp.where(empty, 0.0, head).astype(rows_ref.dtype)
            live = rows_ref.shape[1] - jnp.sum(jnp.where(empty, 1.0, 0.0))
            squares = jnp.zeros((8, width), jnp.float32)
            for part in range(parts):
                block = rows_ref[expert, part * capacity : (part + 1) * capacity].astype(jnp.float32)
                squares = squares + jnp.sum((block * block).reshape(-1, 8, width), axis=0)
            scale = 2.0 / live
            stat_ref[0] = scale
            stat_ref[1] = 0.1 * (jnp.sum(squares) * scale / width)

    first = side_ref[0] * half + place * tile
    left = rows_ref[local, :, pl.ds(pl.multiple_of(first, LANES), tile)]
    gram = lax.dot_general(
        left, rows_ref[local], (((0,), (0,)), ((), ())), preferred_element_type=jnp.float32
    )
    row = lax.broadcasted_iota(jnp.int32, gram.shape, 0) + first
    col = lax.broadcasted_iota(jnp.int32, gram.shape, 1)
    out_ref[0] = gram * stat_ref[0] + jnp.where(row == col, stat_ref[1], 0.0)


def hessians(side, chunks, capacity, half):
    width = chunks[0].shape[1]
    parts = len(chunks)
    tile = 256
    tiles = half // tile
    any_space = pl.BlockSpec(memory_space=pl.ANY)
    return pl.pallas_call(
        functools.partial(hessian_kernel, parts, capacity, half, tile),
        grid=(EXP_DEV * tiles,),
        out_shape=jax.ShapeDtypeStruct((EXP_DEV, half, width), jnp.float32),
        in_specs=[pl.BlockSpec(memory_space=pltpu.SMEM)] + [any_space] * parts,
        out_specs=pl.BlockSpec((1, tile, width), lambda i: (i // tiles, i % tiles, 0)),
        scratch_shapes=[
            pltpu.VMEM((EXP_DEV, parts * capacity, width), chunks[0].dtype),
            pltpu.SMEM((2,), jnp.float32),
            pltpu.SemaphoreType.DMA((EXP_DEV, parts)),
        ],
        name="hessians",
    )(side, *chunks)


def swap(x):
    return lax.ppermute(x, "dp", [(0, 1), (1, 0)])


def body(captured, routes):
    rows_dev, width = captured.shape
    n_owner = lax.axis_size("expert")
    experts = EXP_DEV * n_owner
    capacity = max(2, 5 * rows_dev // (4 * experts))
    half = width // lax.axis_size("dp")
    me = lax.axis_index("expert").astype(jnp.int32).reshape(1)
    side = lax.axis_index("dp").astype(jnp.int32).reshape(1)
    table = routes.reshape(rows_dev // LANES, LANES)
    far = list(range(n_owner // 2, n_owner))[::-1]
    near = list(range(n_owner // 2))
    packed = dict(zip(far, pack(far, experts, capacity, me, table, captured)))
    packed.update(zip(near, pack(near, experts, capacity, me, table, captured)))
    chunks = []
    for offset in [2, 3, 1] + far:
        moved = lax.ppermute(packed[offset], "expert", [(i, i ^ offset) for i in range(n_owner)])
        chunks += [moved, swap(moved)]
    chunks += [packed[0], swap(packed[0])]
    return hessians(side, chunks, capacity, half)


def general_body(captured, routes):
    rows_dev, width = captured.shape
    n_owner = lax.axis_size("expert")
    n_pair = lax.axis_size("dp")
    experts = EXP_DEV * n_owner
    capacity = max(2, 5 * rows_dev // (4 * experts))
    half_width = width // n_pair
    offset_col = lax.axis_index("dp") * half_width
    expert_ids = routes[:, 0]
    onehot = (expert_ids[:, None] == jnp.arange(experts, dtype=jnp.int32)[None, :]).astype(jnp.int32)
    slot_rank = jnp.sum(onehot * jnp.cumsum(onehot, axis=0), axis=1) - 1
    slot_index = expert_ids * capacity + slot_rank
    row_tiles = jnp.zeros((experts * capacity, width), captured.dtype).at[slot_index].set(captured)
    row_tiles = row_tiles.reshape(n_owner, EXP_DEV * capacity, width)
    counts = jnp.sum(onehot, axis=0).reshape(n_owner, EXP_DEV)
    rows = lax.all_to_all(row_tiles, "expert", split_axis=0, concat_axis=0, tiled=True)
    got = lax.all_to_all(counts, "expert", split_axis=0, concat_axis=0, tiled=True)
    rows = lax.all_gather(rows, "dp", axis=0, tiled=True)
    got = lax.all_gather(got, "dp", axis=0, tiled=True)
    totals = jnp.sum(got, axis=0).astype(jnp.float32)
    rows = rows.reshape(rows.shape[0], EXP_DEV, capacity, width)
    on_diagonal = jnp.arange(half_width)[:, None] + offset_col == jnp.arange(width)[None, :]
    outs = []
    for local in range(EXP_DEV):
        block = rows[:, local].reshape(-1, width)
        left = lax.dynamic_slice_in_dim(block, offset_col, half_width, 1)
        gram = lax.dot_general(
            left, block, (((0,), (0,)), ((), ())), preferred_element_type=jnp.float32
        )
        scale = 2.0 / totals[local]
        wide = block.astype(jnp.float32)
        damping = 0.1 * (jnp.sum(wide * wide) * scale / width)
        outs.append(gram * scale + jnp.where(on_diagonal, damping, 0.0))
    return jnp.stack(outs)


def solution(mesh):
    small = mesh.shape["expert"] == 8 and mesh.shape["dp"] == 2
    return jax.shard_map(
        body if small else general_body,
        mesh=mesh,
        in_specs=(P(("groups", "expert", "dp"), None), P(("groups", "expert", "dp"), None)),
        out_specs=P(("groups", "expert"), "dp", None),
        check_vma=False,
    )
```

```python
import functools

import jax
import jax.numpy as jnp
from jax import lax
from jax.experimental import pallas as pl
from jax.experimental.pallas import tpu as pltpu
from jax.sharding import PartitionSpec as P


EXP_DEV = 2
LANES = 128
EMPTY = 64.0
TILE = 256


def slot_codes(routes, experts, capacity):
    blocks = routes.shape[0]
    hits = [routes == expert for expert in range(experts)]
    onehot = jnp.concatenate([hit.astype(jnp.float32) for hit in hits], axis=0).astype(jnp.bfloat16)
    rows = lax.broadcasted_iota(jnp.int32, (LANES, LANES), 0)
    cols = lax.broadcasted_iota(jnp.int32, (LANES, LANES), 1)
    upto = jnp.where(rows <= cols, 1.0, 0.0).astype(jnp.bfloat16)
    ones = jnp.ones((LANES, LANES), jnp.bfloat16)
    within = jnp.dot(onehot, upto, preferred_element_type=jnp.float32)
    totals = jnp.dot(onehot, ones, preferred_element_type=jnp.float32).astype(jnp.bfloat16)
    side = experts * blocks
    left = lax.broadcasted_iota(jnp.int32, (side, side), 0)
    right = lax.broadcasted_iota(jnp.int32, (side, side), 1)
    same = (left // blocks == right // blocks) & (right < left)
    before = jnp.where(same, 1.0, 0.0).astype(jnp.bfloat16)
    rank = within + jnp.dot(before, totals, preferred_element_type=jnp.float32) - 1.0
    code = jnp.zeros(routes.shape, jnp.float32)
    for expert in range(experts):
        own = rank[expert * blocks : (expert + 1) * blocks]
        code = jnp.where(hits[expert], own + float(expert * capacity), code)
    return code.astype(jnp.int32)


def select_rows(code, firsts, captured_ref, columns, out_refs):
    blocks = code.shape[0]
    picks = []
    for first, out_ref in zip(firsts, out_refs):
        wanted = lax.broadcasted_iota(jnp.int32, (out_ref.shape[0], LANES), 0) + first
        row = [
            jnp.where(code[block : block + 1] == wanted, 1.0, 0.0).astype(jnp.bfloat16)
            for block in range(blocks)
        ]
        picks.append(jnp.concatenate(row, axis=1))
    pick = jnp.concatenate(picks, axis=0)
    captured = captured_ref[:, columns]
    packed = jnp.dot(pick, captured, preferred_element_type=jnp.float32).astype(jnp.bfloat16)
    if columns.start == 0:
        ones = jnp.ones((captured.shape[0], LANES), jnp.bfloat16)
        filled = jnp.dot(pick, ones, preferred_element_type=jnp.float32)
        lane = lax.broadcasted_iota(jnp.int32, filled.shape, 1)
        empty = (filled < 0.5) & (lane == 0)
        head = jnp.where(empty, EMPTY, packed[:, :LANES].astype(jnp.float32)).astype(jnp.bfloat16)
    else:
        head = packed[:, :LANES]
    start = 0
    for out_ref in out_refs:
        stop = start + out_ref.shape[0]
        out_ref[:, :LANES] = head[start:stop]
        out_ref[:, LANES:] = packed[start:stop, LANES:]
        start = stop


def pack_kernel(pieces, experts, capacity, me_ref, routes_hbm, captured_hbm, *refs):
    out_refs, (routes_ref, captured_ref, sems) = refs[: len(pieces)], refs[len(pieces) :]
    loaded = captured_ref.shape[1]
    copies = [
        pltpu.make_async_copy(routes_hbm, routes_ref, sems.at[0]),
        pltpu.make_async_copy(captured_hbm.at[:, pl.ds(0, loaded)], captured_ref, sems.at[1]),
    ]
    for copy in copies:
        copy.start()
    copies[0].wait()
    code = slot_codes(routes_ref[...], experts, capacity)
    copies[1].wait()
    for columns in sorted({(piece[3], piece[4]) for piece in pieces}):
        mine = [i for i, piece in enumerate(pieces) if (piece[3], piece[4]) == columns]
        firsts = [
            ((me_ref[0] ^ pieces[i][0]) * EXP_DEV + pieces[i][1]) * capacity for i in mine
        ]
        select_rows(code, firsts, captured_ref, slice(*columns), [out_refs[i] for i in mine])


def pack(pieces, experts, capacity, me, routes, captured, limit):
    rows, _ = captured.shape
    outs = [
        jax.ShapeDtypeStruct((piece[2] * capacity, piece[4] - piece[3]), captured.dtype)
        for piece in pieces
    ]
    work = rows * sum(out.shape[0] * out.shape[1] for out in outs)
    vmem = pl.BlockSpec(memory_space=pltpu.VMEM)
    hbm = pl.BlockSpec(memory_space=pltpu.HBM)
    loaded = max(piece[4] for piece in pieces)
    return pl.pallas_call(
        functools.partial(pack_kernel, pieces, experts, capacity),
        out_shape=outs,
        in_specs=[pl.BlockSpec(memory_space=pltpu.SMEM), hbm, hbm],
        out_specs=[vmem] * len(outs),
        scratch_shapes=[
            pltpu.VMEM(routes.shape, routes.dtype),
            pltpu.VMEM((rows, loaded), captured.dtype),
            pltpu.SemaphoreType.DMA((2,)),
        ],
        compiler_params=pltpu.CompilerParams(vmem_limit_bytes=limit),
        cost_estimate=pl.CostEstimate(
            flops=2 * work, bytes_accessed=2 * (rows * loaded + work // rows), transcendentals=0
        ),
        name="pack",
    )(me, routes, captured)


def row_sums(rows_ref, capacity):
    width = rows_ref.shape[1]
    head = rows_ref[:, :LANES].astype(jnp.float32)
    empty = head > 0.5 * EMPTY
    rows_ref[:, :LANES] = jnp.where(empty, 0.0, head).astype(rows_ref.dtype)
    live = rows_ref.shape[0] - jnp.sum(jnp.where(empty, 1.0, 0.0))
    squares = jnp.zeros((8, width), jnp.float32)
    for first in range(0, rows_ref.shape[0], capacity):
        block = rows_ref[first : first + capacity].astype(jnp.float32)
        squares = squares + jnp.sum((block * block).reshape(-1, 8, width), axis=0)
    return live, jnp.sum(squares)


def load_rows(places, capacity, part_refs, rows_ref, sems):
    copies = [
        pltpu.make_async_copy(
            part_ref.at[pl.ds(first, capacity)],
            rows_ref.at[pl.ds(row, capacity), pl.ds(column, part_ref.shape[1])],
            sems.at[part],
        )
        for part, ((row, column, first), part_ref) in enumerate(zip(places, part_refs))
    ]
    for copy in copies:
        copy.start()
    for copy in copies:
        copy.wait()


def gram_tile(first, tile, rows_ref):
    left = rows_ref[:, pl.ds(pl.multiple_of(first, LANES), tile)]
    return lax.dot_general(
        left, rows_ref[...], (((0,), (0,)), ((), ())), preferred_element_type=jnp.float32
    )


def damped(gram, first, stat_ref):
    row = lax.broadcasted_iota(jnp.int32, gram.shape, 0) + first
    col = lax.broadcasted_iota(jnp.int32, gram.shape, 1)
    return gram * stat_ref[0] + jnp.where(row == col, stat_ref[1], 0.0)


def whole_kernel(places, capacity, side_ref, *refs):
    parts = len(places)
    part_refs, out_ref, rows_ref, sems, stat_ref = refs[:parts], refs[parts], *refs[parts + 1 :]
    _, tile, width = out_ref.shape
    step = pl.program_id(0)

    @pl.when(step == 0)
    def _():
        load_rows(places, capacity, part_refs, rows_ref, sems)
        live, squares = row_sums(rows_ref, capacity)
        stat_ref[0] = 2.0 / live
        stat_ref[1] = 0.1 * (squares * (2.0 / live) / width)

    first = (side_ref[0] * pl.num_programs(0) + step) * tile
    out_ref[0] = damped(gram_tile(first, tile, rows_ref), first, stat_ref)


def early_kernel(places, capacity, side_ref, *refs):
    parts = len(places)
    part_refs, out_ref, sum_ref, rows_ref, sems = refs[:parts], *refs[parts:]
    tile = out_ref.shape[0]
    step = pl.program_id(0)

    @pl.when(step == 0)
    def _():
        load_rows(places, capacity, part_refs, rows_ref, sems)
        sum_ref[0], sum_ref[1] = row_sums(rows_ref, capacity)

    first = (side_ref[0] * pl.num_programs(0) + step) * tile
    out_ref[...] = gram_tile(first, tile, rows_ref)


def onto_kernel(places, capacity, side_ref, before_ref, early_ref, *refs):
    parts = len(places)
    part_refs, out_ref, sum_ref, rows_ref, sems = refs[:parts], *refs[parts:]
    half = out_ref.shape[0]
    load_rows(places, capacity, part_refs, rows_ref, sems)
    live, squares = row_sums(rows_ref, capacity)
    sum_ref[0] = before_ref[0] + live
    sum_ref[1] = before_ref[1] + squares
    for start in range(0, half, TILE):
        gram = gram_tile(side_ref[0] * half + start, TILE, rows_ref)
        out_ref[start : start + TILE] = early_ref[start : start + TILE] + gram


def final_kernel(places, capacity, side_ref, sum_ref, early_ref, done_ref, *refs):
    parts = len(places)
    part_refs, out_ref, rows_ref, sems, tiles_ref, out_sems = refs[:parts], *refs[parts:]
    half, width = tiles_ref.shape
    load_rows(places, capacity, part_refs, rows_ref, sems)
    live, squares = row_sums(rows_ref, capacity)
    scale = 2.0 / (live + sum_ref[0])
    damping = 0.1 * ((squares + sum_ref[1]) * scale / width)
    row = lax.broadcasted_iota(jnp.int32, (LANES, LANES), 0)
    col = lax.broadcasted_iota(jnp.int32, (LANES, LANES), 1)
    unit = jnp.where(row == col, damping, 0.0)
    copies = []
    for start in range(0, half, LANES):
        first = pl.multiple_of(side_ref[0] * half + start, LANES)
        rows, own = pl.ds(start, LANES), pl.ds(first, LANES)
        tiles_ref[rows] = (gram_tile(first, LANES, rows_ref) + early_ref[rows]) * scale
        tiles_ref[rows, own] = tiles_ref[rows, own] + unit
        copies.append(
            pltpu.make_async_copy(
                tiles_ref.at[rows], out_ref.at[EXP_DEV - 1, rows], out_sems.at[start // LANES]
            )
        )
        copies[-1].start()
    for copy in copies:
        copy.wait()


def call_kernel(kernel, parts, capacity, half, grid, ins, in_specs, outs, out_specs, more, aliases):
    places = [(i * capacity, *piece[:2]) for i, part in enumerate(parts) for piece in part]
    arrays = [piece[2] for part in parts for piece in part]
    width = sum(piece[2].shape[1] for piece in parts[0])
    rows = len(parts) * capacity
    scratch = [pltpu.VMEM((rows, width), arrays[0].dtype), pltpu.SemaphoreType.DMA((len(arrays),))]
    return pl.pallas_call(
        functools.partial(kernel, places, capacity),
        grid=(grid,) if grid else (),
        out_shape=outs,
        in_specs=in_specs + [pl.BlockSpec(memory_space=pl.ANY)] * len(arrays),
        out_specs=out_specs,
        scratch_shapes=scratch + more,
        input_output_aliases=aliases,
        compiler_params=pltpu.CompilerParams(vmem_limit_bytes=24 << 20),
        cost_estimate=pl.CostEstimate(
            flops=2 * rows * half * width,
            bytes_accessed=2 * rows * width + 4 * half * width,
            transcendentals=0,
        ),
    )(*ins, *arrays)


def far_offsets(n_owner):
    return list(range(n_owner // 2, n_owner))[::-1]


def near_offsets(n_owner):
    return list(range(n_owner // 2))[::-1]


def pieces_of(n_owner, width):
    far, near = far_offsets(n_owner), near_offsets(n_owner)
    split = width // 2 // LANES * LANES
    first = [(offset, 0, 1, 0, split) for offset in far]
    other = [(offset, 0, 1, split, width) for offset in far]
    other += [(offset, 0, EXP_DEV, 0, width) for offset in near]
    other += [(offset, 1, 1, 0, width) for offset in far]
    return first, other


def body(captured, routes):
    return routed_hessians(captured, routes)


def routed_hessians(captured, routes):
    rows_dev, width = captured.shape
    n_owner = lax.axis_size("expert")
    experts = EXP_DEV * n_owner
    capacity = max(2, 5 * rows_dev // (4 * experts))
    half = width // lax.axis_size("dp")
    me = lax.axis_index("expert").astype(jnp.int32).reshape(1)
    side = lax.axis_index("dp").astype(jnp.int32).reshape(1)
    table = routes.reshape(rows_dev // LANES, LANES)
    first, other = pieces_of(n_owner, width)
    packed = []
    for pieces, limit in ((first, 62 << 20), (other, 62 << 20)):
        packed += zip(pieces, pack(pieces, experts, capacity, me, table, captured, limit))
    parts = {}
    for piece, rows in packed:
        offset, expert, number, column, _ = piece
        if offset:
            rows = lax.ppermute(rows, "expert", [(i, i ^ offset) for i in range(n_owner)])
        other = lax.ppermute(rows, "dp", [(0, 1), (1, 0)])
        for source, part in enumerate((rows, other)):
            for i in range(number):
                key = (expert + i, offset, source)
                parts.setdefault(key, []).append((column, i * capacity, part))

    def rows_of(expert, offsets):
        return [parts[expert, offset, source] for offset in offsets for source in range(2)]

    tile = TILE
    smem = pl.BlockSpec(memory_space=pltpu.SMEM)
    vmem = pl.BlockSpec(memory_space=pltpu.VMEM)
    hbm = pl.BlockSpec(memory_space=pl.ANY)
    out = jax.ShapeDtypeStruct((EXP_DEV, half, width), jnp.float32)
    gram = [jax.ShapeDtypeStruct((half, width), jnp.float32), jax.ShapeDtypeStruct((2,), jnp.float32)]
    far, near = far_offsets(n_owner), near_offsets(n_owner)
    done = call_kernel(
        whole_kernel, rows_of(0, far + near), capacity, half, half // tile, [side], [smem],
        out, pl.BlockSpec((1, tile, width), lambda i: (0, i, 0)), [pltpu.SMEM((2,), jnp.float32)], {},
    )
    early, sums = call_kernel(
        early_kernel, rows_of(1, near), capacity, half, half // tile, [side], [smem],
        gram, [pl.BlockSpec((tile, width), lambda i: (i, 0)), smem], [], {},
    )
    for offsets in (far[:-2], far[-2:-1]):
        early, sums = call_kernel(
            onto_kernel, rows_of(1, offsets), capacity, half, 0, [side, sums, early],
            [smem, smem, vmem], gram, [vmem, smem], [], {2: 0},
        )
    tiles = [pltpu.VMEM((half, width), jnp.float32), pltpu.SemaphoreType.DMA((half // LANES,))]
    return call_kernel(
        final_kernel, rows_of(1, far[-1:]), capacity, half, 0, [side, sums, early, done],
        [smem, smem, vmem, hbm], out, hbm, tiles, {3: 0},
    )


def general_body(captured, routes):
    rows_dev, width = captured.shape
    n_owner = lax.axis_size("expert")
    n_pair = lax.axis_size("dp")
    experts = EXP_DEV * n_owner
    capacity = max(2, 5 * rows_dev // (4 * experts))
    half_width = width // n_pair
    offset_col = lax.axis_index("dp") * half_width
    expert_ids = routes[:, 0]
    onehot = (expert_ids[:, None] == jnp.arange(experts, dtype=jnp.int32)[None, :]).astype(jnp.int32)
    slot_rank = jnp.sum(onehot * jnp.cumsum(onehot, axis=0), axis=1) - 1
    slot_index = expert_ids * capacity + slot_rank
    row_tiles = jnp.zeros((experts * capacity, width), captured.dtype).at[slot_index].set(captured)
    row_tiles = row_tiles.reshape(n_owner, EXP_DEV * capacity, width)
    counts = jnp.sum(onehot, axis=0).reshape(n_owner, EXP_DEV)
    rows = lax.all_to_all(row_tiles, "expert", split_axis=0, concat_axis=0, tiled=True)
    got = lax.all_to_all(counts, "expert", split_axis=0, concat_axis=0, tiled=True)
    rows = lax.all_gather(rows, "dp", axis=0, tiled=True)
    got = lax.all_gather(got, "dp", axis=0, tiled=True)
    totals = jnp.sum(got, axis=0).astype(jnp.float32)
    rows = rows.reshape(rows.shape[0], EXP_DEV, capacity, width)
    on_diagonal = jnp.arange(half_width)[:, None] + offset_col == jnp.arange(width)[None, :]
    outs = []
    for local in range(EXP_DEV):
        block = rows[:, local].reshape(-1, width)
        left = lax.dynamic_slice_in_dim(block, offset_col, half_width, 1)
        gram = lax.dot_general(
            left, block, (((0,), (0,)), ((), ())), preferred_element_type=jnp.float32
        )
        scale = 2.0 / totals[local]
        wide = block.astype(jnp.float32)
        damping = 0.1 * (jnp.sum(wide * wide) * scale / width)
        outs.append(gram * scale + jnp.where(on_diagonal, damping, 0.0))
    return jnp.stack(outs)


def solution(mesh):
    small = mesh.shape["expert"] == 8 and mesh.shape["dp"] == 2
    return jax.shard_map(
        body if small else general_body,
        mesh=mesh,
        in_specs=(P(("groups", "expert", "dp"), None), P(("groups", "expert", "dp"), None)),
        out_specs=P(("groups", "expert"), "dp", None),
        check_vma=False,
    )
```
